256 devices in a mesh: blk: 16 (over z_hi, y), grp: 16 (over z_lo, x, core).
Axes of the slice: x: 4, y: 4, z: 8 (z_hi: 4, z_lo: 2; z = z_hi * 2 + z_lo), core: 2. Of those that a mesh axis runs over, the one named last changes fastest.
Arguments:
- tiles: bfloat16 [1024, 20, 128, 128], P(('blk', 'grp')), may hold values from -1 to 3.5
- columns: int32 [1024, 20], P(('blk', 'grp')), may hold values from -1 to 1023, as said below
Outputs:
- square: bfloat16 [1024, 20, 128, 128], P(('blk', 'grp'))
- trace_mean: float32 [], replicated
The draws below stay inside these ranges and needn't reach their ends.
Inputs may be any that keep to these rules, and one draw needn't show every extreme that they name: Slot 0 of row i holds i. The filled slots of a row come first, then -1. The filled columns of a row are distinct and lie within 12 block rows of i, counted periodically modulo 1024. Every device has a row with all 20 slots filled that reaches i - 12 and one that reaches i + 12.
All inputs are finite; a program needn't handle non-finite values.
Results may differ from the reference program's by a relative error of at most 0.001.
Values may be sent and summed in bfloat16 or wider, within the bound.
A program may use at most 192 MiB of HBM per device.

```python
import jax
import jax.numpy as jnp
from jax import lax

BS = 128
NNZ = 20
REACH = 12
R_DEV = 4
NB = 1024


def draw_tiles(key, part):
    entry_key, gain_key = jax.random.split(jax.random.fold_in(key, 11))
    entries = jnp.clip(0.14 * jax.random.normal(entry_key, (NB, NNZ, BS, BS), jnp.float32), -0.8, 0.8)
    row_ramp = 1.0 + 0.7 * jnp.arange(NB, dtype=jnp.float32) / NB
    spread = jnp.exp(jax.random.uniform(gain_key, (NB, BS), jnp.float32, -0.3, 0.3))
    diagonal_gain = row_ramp[:, None] * spread
    identity = jnp.eye(BS, dtype=jnp.float32)
    entries = entries.at[:, 0].add(diagonal_gain[:, :, None] * identity[None])
    return entries.astype(jnp.bfloat16)


def draw_columns(key, part):
    count_key, score_key = jax.random.split(jax.random.fold_in(key, 23))
    row_index = jnp.arange(NB, dtype=jnp.int32)
    full_rows = (row_index % R_DEV == 0) | (row_index % R_DEV == R_DEV - 1)
    counts = jax.random.randint(count_key, (NB,), NNZ // 2, NNZ + 1, dtype=jnp.int32)
    counts = jnp.where(full_rows, NNZ, counts)
    candidates = jnp.concatenate([jnp.arange(-REACH, 0, dtype=jnp.int32), jnp.arange(1, REACH + 1, dtype=jnp.int32)])
    width_count = 2 * REACH
    scores = jax.random.randint(score_key, (NB, width_count), 0, 1 << 20, dtype=jnp.int32) * width_count + jnp.arange(width_count, dtype=jnp.int32)[None, :]
    forced = scores.at[:, 0].set(-2).at[:, width_count - 1].set(-1)
    scores = jnp.where(full_rows[:, None], forced, scores)
    order = jnp.argsort(scores, axis=1, stable=True)
    chosen = candidates[order][:, :NNZ - 1]
    others = jnp.mod(row_index[:, None] + chosen, NB).astype(jnp.int32)
    slot_ids = jnp.arange(1, NNZ, dtype=jnp.int32)
    others = jnp.where(slot_ids[None, :] < counts[:, None], others, -1)
    return jnp.concatenate([row_index[:, None], others], axis=1).astype(jnp.int32)


def setup_inputs(seed: int = 0) -> dict:
    splits = jax.random.split(jax.random.key(seed), 3)
    return {
        "tiles": draw_tiles(jax.random.fold_in(splits[2], 71), 0),
        "columns": draw_columns(jax.random.fold_in(splits[2], 71), 0),
    }


def reference(tiles, columns):
    all_rows = tiles.shape[0]
    slots_count = tiles.shape[1]
    block_size = tiles.shape[2]
    flat_tiles = tiles.reshape(all_rows * slots_count, block_size, block_size)
    slot_ids = jnp.arange(slots_count, dtype=jnp.int32)

    def one_row(inputs):
        own_tiles, row_cols = inputs
        filled = row_cols >= 0
        position = jnp.where(filled, row_cols, 0).astype(jnp.int32)
        far_cols = columns[position]
        matches = (far_cols[:, None, :] == row_cols[None, :, None]) & filled[:, None, None] & filled[None, :, None]
        found = jnp.any(matches, axis=2)
        which_slot = jnp.sum(jnp.where(matches, slot_ids[None, None, :], 0), axis=2).astype(jnp.int32)
        flat_index = (position[:, None] * slots_count + which_slot).astype(jnp.int32)
        panel = jnp.where(found[:, :, None, None], flat_tiles[flat_index], jnp.zeros((), tiles.dtype))
        product = jnp.einsum("tab,tsbc->sac", own_tiles.astype(jnp.float32), panel.astype(jnp.float32))
        return product.astype(jnp.bfloat16), jnp.trace(product[0])

    square, traces = lax.map(one_row, (tiles, columns))
    trace_mean = jnp.sum(traces) / (all_rows * block_size)
    return square, trace_mean
```

```python
import functools

import jax
import jax.numpy as jnp
from jax import lax
from jax.experimental import pallas as pl
from jax.experimental.pallas import tpu as pltpu
from jax.sharding import PartitionSpec as P

REACH = 12
R = 4
BS = 128
COLS = 2 * REACH + R
MESH = pl.DeviceIdType.MESH


def spread_kernel(pos_ref, tiles_ref, dense_ref):
    dense_ref[...] = jnp.zeros_like(dense_ref)
    slots = tiles_ref.shape[1]
    for r in range(R):
        def place(s, carry, r=r):
            p = pos_ref[r, s]

            @pl.when(p >= 0)
            def _():
                dense_ref[r, p] = tiles_ref[r, s]

            return carry

        lax.fori_loop(0, slots, place, 0)


def square_kernel(n_blk, n_grp, pos_ref, own, square_ref, trace_ref,
                  out1, out2, out3, in1, in2, in3, acc, send_sem, recv_sem):
    n = n_blk * n_grp
    me = lax.axis_index("blk") * n_grp + lax.axis_index("grp")
    odd = lax.rem(me, 2)
    even = 1 - odd
    sign = 2 * odd - 1

    def dev(offset):
        d = lax.rem(me + offset + n, n)
        return (d // n_grp, lax.rem(d, n_grp))

    partner = dev(-sign)
    across = dev(sign)
    onward = dev(-2 * sign)
    behind = dev(2 * sign)

    barrier = pltpu.get_barrier_semaphore()
    for d in (partner, across, onward, behind):
        pl.semaphore_signal(barrier, inc=1, device_id=d, device_id_type=MESH)

    zero = jnp.zeros((BS, BS), jnp.bfloat16)
    for buf, delta, left in ((out1, 1, even), (out2, 2, even), (out3, 3, even),
                             (in1, 1, odd), (in2, 2, odd), (in3, 3, odd)):
        for rho in range(R - 1):
            row = left * rho + (1 - left) * (R - 1 - rho)
            first = left * (25 - 4 * delta + rho)
            for e in range(R - 1 - rho):
                buf[row, first + e] = zero
    pl.semaphore_wait(barrier, 4)

    def send(k, rho, src, src_left, length, dst, device, left):
        row = left * rho + (1 - left) * (R - 1 - rho)
        first = left * src_left + (1 - left) * (R - 1 - rho)
        to = (1 - left) * (R - 1 - rho)
        return pltpu.make_async_remote_copy(
            src_ref=src.at[row, pl.ds(first, length)],
            dst_ref=dst.at[row, pl.ds(to, length)],
            send_sem=send_sem.at[k, rho],
            recv_sem=recv_sem.at[k, rho],
            device_id=device,
            device_id_type=MESH,
        )

    def arrival(k, rho, buf, delta, left):
        length = 25 - 4 * delta + rho
        row = left * rho + (1 - left) * (R - 1 - rho)
        to = (1 - left) * (R - 1 - rho)
        here = buf.at[row, pl.ds(to, length)]
        return pltpu.make_async_copy(here, here, recv_sem.at[k, rho])

    sends = []

    def start(*args):
        c = send(*args)
        c.start()
        sends.append(c)

    order = (3, 2, 1, 0)
    for rho in order:
        start(0, rho, own, 4, 21 + rho, out1, across, odd)
    for rho in order:
        start(1, rho, own, 8, 17 + rho, out2, onward, even)
    for rho in order:
        start(3, rho, own, 4, 21 + rho, in1, partner, even)

    def product(buf, cols, left, delta, first=False):
        a0 = REACH + 4 * delta * (1 - 2 * left)
        c0 = (1 - left) * 4 * delta

        def step(t, carry):
            c = 2 * t
            lhs = jnp.concatenate([own[:, a0 + r].reshape(R * BS, BS) for r in range(R)], axis=1)
            rhs = jnp.concatenate([buf[:, c].reshape(R * BS, BS), buf[:, c + 1].reshape(R * BS, BS)], axis=1)
            res = jnp.dot(lhs, rhs, preferred_element_type=jnp.float32)
            for h in range(2):
                part = res[:, h * BS:(h + 1) * BS].reshape(R, BS, BS)
                if first:
                    acc[:, c0 + c + h] = part
                else:
                    acc[:, c0 + c + h] += part
            return carry

        lax.fori_loop(0, cols // 2, step, 0)

    product(own, 28, even, 0, first=True)
    for rho in order:
        arrival(3, rho, in1, 1, odd).wait()
    product(in1, 24, odd, 1)
    for rho in order:
        arrival(0, rho, out1, 1, even).wait()
        start(2, rho, out1, 8, 13 + rho, out3, onward, even)
        start(4, rho, out1, 4, 17 + rho, in2, partner, even)
        arrival(1, rho, out2, 2, even).wait()
        start(5, rho, out2, 4, 13 + rho, in3, partner, even)
    product(out2, 20, even, 2)
    product(out1, 24, even, 1)
    for rho in order:
        arrival(5, rho, in3, 3, odd).wait()
    product(in3, 16, odd, 3)
    for rho in order:
        arrival(4, rho, in2, 2, odd).wait()
    product(in2, 20, odd, 2)
    for rho in order:
        arrival(2, rho, out3, 3, even).wait()
    product(out3, 16, even, 3)

    for r in range(R):
        def take(s, carry, r=r):
            p = pos_ref[r, s]
            tile = acc[r, jnp.maximum(p, 0)]
            square_ref[r, s] = jnp.where(p >= 0, tile, 0.0).astype(jnp.bfloat16)
            return carry

        lax.fori_loop(0, square_ref.shape[1], take, 0)

    diagonal = sum(acc[r, REACH + r] for r in range(R))
    rows = lax.broadcasted_iota(jnp.int32, (BS, BS), 0)
    lanes = lax.broadcasted_iota(jnp.int32, (BS, BS), 1)
    diagonal = jnp.where(rows == lanes, diagonal, 0.0)
    trace_ref[...] = jnp.sum(diagonal.reshape(BS // 8, 8, BS), axis=0)

    for c in sends:
        c.wait_send()


def shards(tiles, columns, n_blk, n_grp):
    n = n_blk * n_grp
    all_rows = n * R
    me = lax.axis_index("blk") * n_grp + lax.axis_index("grp")
    pos = jnp.where(columns >= 0, jnp.mod(columns - me * R + REACH, all_rows), -1)
    dense = pl.pallas_call(
        spread_kernel,
        out_shape=jax.ShapeDtypeStruct((R, COLS, BS, BS), jnp.bfloat16),
        in_specs=[pl.BlockSpec(memory_space=pltpu.SMEM), pl.BlockSpec(memory_space=pltpu.VMEM)],
        out_specs=pl.BlockSpec(memory_space=pltpu.VMEM),
    )(pos, tiles)
    piece = lambda delta: pltpu.VMEM((R, COLS - 4 * delta, BS, BS), jnp.bfloat16)
    square, partial = pl.pallas_call(
        functools.partial(square_kernel, n_blk, n_grp),
        out_shape=(
            jax.ShapeDtypeStruct(tiles.shape, jnp.bfloat16),
            jax.ShapeDtypeStruct((8, BS), jnp.float32),
        ),
        in_specs=[pl.BlockSpec(memory_space=pltpu.SMEM), pl.BlockSpec(memory_space=pltpu.VMEM)],
        out_specs=(pl.BlockSpec(memory_space=pltpu.VMEM), pl.BlockSpec(memory_space=pltpu.VMEM)),
        scratch_shapes=[
            piece(1), piece(2), piece(3), piece(1), piece(2), piece(3),
            pltpu.VMEM((R, COLS, BS, BS), jnp.float32),
            pltpu.SemaphoreType.DMA((6, R)),
            pltpu.SemaphoreType.DMA((6, R)),
        ],
        compiler_params=pltpu.CompilerParams(
            collective_id=0, has_side_effects=True, vmem_limit_bytes=56 * 2**20
        ),
    )(pos, dense)
    total = lax.psum(jnp.sum(partial), ("blk", "grp"))
    return square, total / (all_rows * BS)


def solution(mesh):
    n_blk, n_grp = mesh.shape["blk"], mesh.shape["grp"]
    return jax.shard_map(
        functools.partial(shards, n_blk=n_blk, n_grp=n_grp),
        mesh=mesh,
        in_specs=(P(("blk", "grp"), None, None, None), P(("blk", "grp"), None)),
        out_specs=(P(("blk", "grp"), None, None, None), P()),
        check_vma=False,
    )
```

```python
import functools

import jax
import jax.numpy as jnp
from jax import lax
from jax.experimental import pallas as pl
from jax.experimental.pallas import tpu as pltpu
from jax.sharding import PartitionSpec as P

REACH = 12
R = 4
BS = 128
COLS = 2 * REACH + R
MESH = pl.DeviceIdType.MESH
X_CHIPS = 4
ORDER = (3, 2, 1, 0)


def xor_strides(n):
    strides = []
    stride = 2 * X_CHIPS
    while stride < n:
        strides.append(stride)
        stride *= 2
    return strides


def square_kernel(n_blk, n_grp, columns_ref, tiles, square_ref, trace_ref,
                  own, out1, out2, out3, in1, in2, in3, acc, sent, got,
                  send_sem, recv_sem, sum_send_sem, sum_recv_sem):
    n = n_blk * n_grp
    slots = tiles.shape[1]
    me = lax.axis_index("blk") * n_grp + lax.axis_index("grp")
    odd = lax.rem(me, 2)
    even = 1 - odd
    sign = 2 * odd - 1

    def coords(d):
        return (d // n_grp, lax.rem(d, n_grp))

    def dev(offset):
        return coords(lax.rem(me + offset + n, n))

    partner = dev(-sign)
    across = dev(sign)
    onward = dev(-2 * sign)
    behind = dev(2 * sign)

    x = lax.rem(me // 2, X_CHIPS)
    ring_to = coords(me + 2 * (lax.rem(x + sign + X_CHIPS, X_CHIPS) - x))
    ring_from = coords(me + 2 * (lax.rem(x - sign + X_CHIPS, X_CHIPS) - x))
    mirrors = [coords(me + w * (1 - 2 * lax.rem(me // w, 2))) for w in xor_strides(n)]

    barrier = pltpu.get_barrier_semaphore()
    greeted = [partner, across, onward, behind, ring_to, ring_from] + mirrors
    for d in greeted:
        pl.semaphore_signal(barrier, inc=1, device_id=d, device_id_type=MESH)

    zero = jnp.zeros((BS, BS), jnp.bfloat16)
    for buf, delta, left in ((out1, 1, even), (out2, 2, even), (out3, 3, even),
                             (in1, 1, odd), (in2, 2, odd), (in3, 3, odd)):
        for rho in range(R - 1):
            row = left * rho + (1 - left) * (R - 1 - rho)
            first = left * (25 - 4 * delta + rho)
            for e in range(R - 1 - rho):
                buf[row, first + e] = zero

    def position(r, s):
        column = columns_ref[r, s]
        p = column - me * R + REACH
        p = jnp.where(p < 0, p + n * R, p)
        p = jnp.where(p >= n * R, p - n * R, p)
        return jnp.where(column >= 0, p, -1)

    def spread(r):
        filled = [position(r, s) for s in range(slots)]

        def place(p, carry):
            s = 0
            for k, f in enumerate(filled):
                s = jnp.where(f == p, k + 1, s)
            tile = tiles[r, jnp.maximum(s - 1, 0)]
            own[r, p] = jnp.where(s > 0, tile, zero)
            return carry

        lax.fori_loop(0, COLS, place, 0)

    sends = []

    def start(k, rho, src, first, dst, to, length, device, left):
        row = left * rho + (1 - left) * (R - 1 - rho)
        c = pltpu.make_async_remote_copy(
            src_ref=src.at[row, pl.ds(left * first[0] + (1 - left) * first[1], length)],
            dst_ref=dst.at[row, pl.ds(left * to[0] + (1 - left) * to[1], length)],
            send_sem=send_sem.at[k, rho],
            recv_sem=recv_sem.at[k, rho],
            device_id=device,
            device_id_type=MESH,
        )
        c.start()
        sends.append(c)

    def arrived(k, rho, buf, to, length, left):
        row = left * rho + (1 - left) * (R - 1 - rho)
        here = buf.at[row, pl.ds(left * to[0] + (1 - left) * to[1], length)]
        pltpu.make_async_copy(here, here, recv_sem.at[k, rho]).wait()

    def send_out1(rho):
        start(0, rho, own, (4, 3 - rho), out1, (0, 3 - rho), 21 + rho, across, odd)

    def send_in1(rho):
        start(3, rho, own, (4, 3 - rho), in1, (0, 3 - rho), 21 + rho, partner, even)

    def send_out2(rho):
        start(1, rho, own, (8, 4), out2, (0, 4), 16, onward, even)

    def send_out2_trace(rho):
        start(6, rho, own, (24, 3 - rho), out2, (16, 3 - rho), rho + 1, onward, even)

    def send_out3(rho):
        start(2, rho, out1, (8, 3 - rho), out3, (0, 3 - rho), 13 + rho, onward, even)

    def send_in2(rho):
        start(4, rho, out1, (4, 3 - rho), in2, (0, 3 - rho), 17 + rho, partner, even)

    def send_in3(rho):
        start(5, rho, out2, (4, 3 - rho), in3, (0, 3 - rho), 13 + rho, partner, even)

    def have_out1(rho):
        arrived(0, rho, out1, (0, 3 - rho), 21 + rho, even)

    def have_out2(rho):
        arrived(1, rho, out2, (0, 4), 16, even)

    def have_out2_trace(rho):
        arrived(6, rho, out2, (16, 3 - rho), rho + 1, even)

    def have_out3(rho):
        arrived(2, rho, out3, (0, 3 - rho), 13 + rho, even)

    def have_in1(rho):
        arrived(3, rho, in1, (0, 3 - rho), 21 + rho, odd)

    def have_in2(rho):
        arrived(4, rho, in2, (0, 3 - rho), 17 + rho, odd)

    def have_in3(rho):
        arrived(5, rho, in3, (0, 3 - rho), 13 + rho, odd)

    def pass_on(j, src, device):
        c = pltpu.make_async_remote_copy(
            src_ref=src,
            dst_ref=got.at[j],
            send_sem=sum_send_sem.at[j],
            recv_sem=sum_recv_sem.at[j],
            device_id=device,
            device_id_type=MESH,
        )
        c.start()
        sends.append(c)

    def received(j):
        pltpu.make_async_copy(got.at[j], got.at[j], sum_recv_sem.at[j]).wait()

    def product(buf, lo, hi, left, delta, first=False):
        a0 = REACH + 4 * delta * (1 - 2 * left)
        c0 = (1 - left) * 4 * delta

        def step(t, carry):
            c = 2 * t
            lhs = jnp.concatenate([own[:, a0 + r].reshape(R * BS, BS) for r in range(R)], axis=1)
            rhs = jnp.concatenate([buf[:, c].reshape(R * BS, BS), buf[:, c + 1].reshape(R * BS, BS)], axis=1)
            res = jnp.dot(lhs, rhs, preferred_element_type=jnp.float32)
            for h in range(2):
                part = res[:, h * BS:(h + 1) * BS].reshape(R, BS, BS)
                if first:
                    acc[:, c0 + c + h] = part
                else:
                    acc[:, c0 + c + h] += part
            return carry

        lax.fori_loop(lo // 2, hi // 2, step, 0)

    def spread_for_out1(rho):
        spread(odd * rho + even * (R - 1 - rho))

    spread_for_out1(3)
    pl.semaphore_wait(barrier, len(greeted))
    spread_for_out1(2)
    send_out1(3)
    spread_for_out1(1)
    send_out1(2)
    spread_for_out1(0)
    send_out1(1)
    for rho in (3, 2):
        send_in1(rho)
    send_out1(0)
    for rho in ORDER:
        send_out2_trace(rho)
    for rho in (1, 0):
        send_in1(rho)

    product(own, 0, 28, even, 0, first=True)
    for rho in ORDER:
        have_in1(rho)
    product(in1, 0, 24, odd, 1)

    for rho in ORDER:
        have_out1(rho)
        send_in2(rho)
        if rho == 1:
            for later in ORDER:
                send_out2(later)
    for rho in ORDER:
        send_out3(rho)
    product(out1, 0, 24, even, 1)
    for rho in ORDER:
        have_out2_trace(rho)
    for rho in ORDER:
        have_in2(rho)

    total = sum(acc[r, REACH + r] for r in range(R))
    for r in range(R):
        a = [out1[even * r + odd * q, even * (16 + q) + odd * (4 + r)] for q in range(R)]
        b = [in1[even * q + odd * r, even * (4 + r) + odd * (16 + q)] for q in range(R)]
        total += 2.0 * jnp.dot(
            jnp.concatenate(a, axis=1), jnp.concatenate(b, axis=0), preferred_element_type=jnp.float32
        )
    for r in range(R):
        a = [out1[even * r + odd * q, even * (20 + q) + odd * r] for q in range(r + 1)]
        b = [in2[even * q + odd * r, even * r + odd * (16 + q)] for q in range(r + 1)]
        a += [out2[even * r + odd * q, even * (16 + q) + odd * r] for q in range(r + 1)]
        b += [in1[even * q + odd * r, even * r + odd * (20 + q)] for q in range(r + 1)]
        total += jnp.dot(
            jnp.concatenate(a, axis=1), jnp.concatenate(b, axis=0), preferred_element_type=jnp.float32
        )
    rows = lax.broadcasted_iota(jnp.int32, (BS, BS), 0)
    lanes = lax.broadcasted_iota(jnp.int32, (BS, BS), 1)
    total = jnp.where(rows == lanes, total, 0.0)
    sent[0] = jnp.sum(total.reshape(BS // 8, 8, BS), axis=0)

    product(in2, 0, 4, odd, 2)
    pass_on(0, sent.at[0], partner)
    product(in2, 4, 12, odd, 2)
    received(0)
    sent[1] = sent[0] + got[0]
    product(in2, 12, 16, odd, 2)
    pass_on(1, sent.at[1], ring_to)
    product(in2, 16, 20, odd, 2)
    received(1)
    pass_on(2, got.at[1], ring_to)
    have_out2(3)
    send_in3(3)
    received(2)
    pass_on(3, got.at[2], ring_to)
    have_out2(2)
    send_in3(2)
    received(3)
    sent[4] = (sent[1] + got[2]) + (got[1] + got[3])
    have_out2(1)
    send_in3(1)
    last = 4 + len(mirrors)
    work = [
        lambda: (have_out2(0), send_in3(0)),
        lambda: product(out2, 0, 10, even, 2),
        lambda: product(out2, 10, 20, even, 2),
        lambda: [have_in3(rho) for rho in ORDER],
        lambda: product(in3, 0, 6, odd, 3),
        lambda: product(in3, 6, 12, odd, 3),
        lambda: product(in3, 12, 16, odd, 3),
    ]
    for j, mirror in enumerate(mirrors):
        pass_on(4 + j, sent.at[4 + j], mirror)
        if work:
            work.pop(0)()
        received(4 + j)
        sent[5 + j] = sent[4 + j] + got[4 + j]
        if work:
            work.pop(0)()
    for w in work:
        w()
    trace_ref[0, 0] = jnp.sum(sent[last]) * (1.0 / (n * R * BS))

    for rho in ORDER:
        have_out3(rho)
        row = even * rho + odd * (R - 1 - rho)
        top = odd * (R - 1 - rho)
        a0 = REACH + 12 * (1 - 2 * even) + row
        m = rho + 1
        begin = odd * (1 if rho < 2 else 0)
        c0 = odd * 12

        def step(t, carry, rho=rho, row=row, top=top, a0=a0, m=m, c0=c0):
            c = 2 * t
            lhs = own[pl.ds(top, m), a0].reshape(m * BS, BS)
            rhs = jnp.concatenate([out3[row, c], out3[row, c + 1]], axis=1)
            res = jnp.dot(lhs, rhs, preferred_element_type=jnp.float32)
            for h in range(2):
                acc[pl.ds(top, m), c0 + c + h] += res[:, h * BS:(h + 1) * BS].reshape(m, BS, BS)
            return carry

        lax.fori_loop(begin, begin + (7 if rho < 2 else 8), step, 0)
        done = even * rho + odd * (R - 1 - rho)

        def take(s, carry, done=done):
            p = position(done, s)
            tile = acc[done, jnp.clip(p, 0, COLS - 1)]
            square_ref[done, s] = jnp.where(p >= 0, tile, 0.0).astype(jnp.bfloat16)
            return carry

        lax.fori_loop(0, slots, take, 0)

    for c in sends:
        c.wait_send()


def shards(tiles, columns, n_blk, n_grp):
    n = n_blk * n_grp
    slots = tiles.shape[1]
    steps = 5 + len(xor_strides(n))
    piece = lambda delta: pltpu.VMEM((R, COLS - 4 * delta, BS, BS), jnp.bfloat16)
    square, trace_mean = pl.pallas_call(
        functools.partial(square_kernel, n_blk, n_grp),
        out_shape=(
            jax.ShapeDtypeStruct(tiles.shape, jnp.bfloat16),
            jax.ShapeDtypeStruct((1, 1), jnp.float32),
        ),
        in_specs=[
            pl.BlockSpec(memory_space=pltpu.SMEM),
            pl.BlockSpec(memory_space=pltpu.VMEM),
        ],
        out_specs=(pl.BlockSpec(memory_space=pltpu.VMEM), pl.BlockSpec(memory_space=pltpu.SMEM)),
        scratch_shapes=[
            piece(0),
            piece(1), piece(2), piece(3), piece(1), piece(2), piece(3),
            pltpu.VMEM((R, COLS, BS, BS), jnp.float32),
            pltpu.VMEM((steps, 8, BS), jnp.float32),
            pltpu.VMEM((steps, 8, BS), jnp.float32),
            pltpu.SemaphoreType.DMA((7, R)),
            pltpu.SemaphoreType.DMA((7, R)),
            pltpu.SemaphoreType.DMA((steps,)),
            pltpu.SemaphoreType.DMA((steps,)),
        ],
        compiler_params=pltpu.CompilerParams(
            collective_id=0, has_side_effects=True, vmem_limit_bytes=36 * 2**20
        ),
    )(columns, tiles)
    return square, trace_mean[0, 0]


def solution(mesh):
    n_blk, n_grp = mesh.shape["blk"], mesh.shape["grp"]
    return jax.shard_map(
        functools.partial(shards, n_blk=n_blk, n_grp=n_grp),
        mesh=mesh,
        in_specs=(P(("blk", "grp"), None, None, None), P(("blk", "grp"), None)),
        out_specs=(P(("blk", "grp"), None, None, None), P()),
        check_vma=False,
    )
```

```python
import functools

import jax
import jax.numpy as jnp
from jax import lax
from jax.experimental import pallas as pl
from jax.experimental.pallas import tpu as pltpu
from jax.sharding import PartitionSpec as P

REACH = 12
R = 4
BS = 128
COLS = 2 * REACH + R
MESH = pl.DeviceIdType.MESH
ORDER = (3, 2, 1, 0)


def xor_groups(n):
    groups = []
    for bits in ((2, 4), (8, 64, 128), (16, 32)):
        bits = [w for w in bits if w < n]
        if bits:
            groups.append([sum(w for i, w in enumerate(bits) if k >> i & 1) for k in range(1, 2 ** len(bits))])
    return groups


def square_kernel(n_blk, n_grp, columns_hbm, tiles_hbm, square_ref, trace_ref,
                  columns_ref, tiles, own, out1, out2, out3, in1, in2, in3, acc, sent, got,
                  load_sem, send_sem, recv_sem, sum_send_sem, sum_recv_sem):
    n = n_blk * n_grp
    slots = tiles.shape[1]
    me = lax.axis_index("blk") * n_grp + lax.axis_index("grp")
    odd = lax.rem(me, 2)
    even = 1 - odd
    sign = 2 * odd - 1

    loads = [
        pltpu.make_async_copy(columns_hbm, columns_ref, load_sem.at[0]),
        pltpu.make_async_copy(tiles_hbm, tiles, load_sem.at[1]),
    ]
    for c in loads:
        c.start()

    def coords(d):
        return (d // n_grp, lax.rem(d, n_grp))

    def dev(offset):
        return coords(lax.rem(me + offset + n, n))

    partner = dev(-sign)
    across = dev(sign)
    onward = dev(-2 * sign)
    behind = dev(2 * sign)

    def mirror(mask):
        d = me
        w = 1
        while w < n:
            if mask & w:
                d += w * (1 - 2 * lax.rem(me // w, 2))
            w *= 2
        return coords(d)

    groups = [[mirror(mask) for mask in group] for group in xor_groups(n)]

    barrier = pltpu.get_barrier_semaphore()
    greeted = [partner, across, onward, behind] + sum(groups, [])
    for d in greeted:
        pl.semaphore_signal(barrier, inc=1, device_id=d, device_id_type=MESH)

    zero = jnp.zeros((BS, BS), jnp.bfloat16)
    for buf, delta, left in ((out1, 1, even), (out2, 2, even), (out3, 3, even),
                             (in1, 1, odd), (in2, 2, odd), (in3, 3, odd)):
        for rho in range(R - 1):
            row = left * rho + (1 - left) * (R - 1 - rho)
            first = left * (25 - 4 * delta + rho)
            for e in range(R - 1 - rho):
                buf[row, first + e] = zero

    def position(r, s):
        column = columns_ref[r, s]
        p = column - me * R + REACH
        p = jnp.where(p < 0, p + n * R, p)
        p = jnp.where(p >= n * R, p - n * R, p)
        return jnp.where(column >= 0, p, -1)

    def spread(r):
        filled = [position(r, s) for s in range(slots)]

        def place(p, carry):
            s = 0
            for k, f in enumerate(filled):
                s = jnp.where(f == p, k + 1, s)
            tile = tiles[r, jnp.maximum(s - 1, 0)]
            own[r, p] = jnp.where(s > 0, tile, zero)
            return carry

        lax.fori_loop(0, COLS, place, 0)

    sends = {}

    def start(k, rho, src, first, dst, to, length, device, left):
        row = left * rho + (1 - left) * (R - 1 - rho)
        c = pltpu.make_async_remote_copy(
            src_ref=src.at[row, pl.ds(left * first[0] + (1 - left) * first[1], length)],
            dst_ref=dst.at[row, pl.ds(left * to[0] + (1 - left) * to[1], length)],
            send_sem=send_sem.at[k, rho],
            recv_sem=recv_sem.at[k, rho],
            device_id=device,
            device_id_type=MESH,
        )
        c.start()
        sends[k, rho] = c

    def wait_sent(k, rho):
        sends.pop((k, rho)).wait_send()

    def arrived(k, rho, buf, to, length, left):
        row = left * rho + (1 - left) * (R - 1 - rho)
        here = buf.at[row, pl.ds(left * to[0] + (1 - left) * to[1], length)]
        pltpu.make_async_copy(here, here, recv_sem.at[k, rho]).wait()

    def send_out1(rho):
        start(0, rho, own, (4, 3 - rho), out1, (0, 3 - rho), 21 + rho, across, odd)

    def send_in1(rho):
        start(3, rho, own, (4, 3 - rho), in1, (0, 3 - rho), 21 + rho, partner, even)

    def send_out2(rho):
        start(1, rho, own, (8, 4), out2, (0, 4), 16, onward, even)

    def send_out2_trace(rho):
        start(6, rho, own, (24, 3 - rho), out2, (16, 3 - rho), rho + 1, onward, even)

    def send_out3(rho):
        start(2, rho, out1, (8, 3 - rho), out3, (0, 3 - rho), 13 + rho, onward, even)

    def send_in2(rho):
        start(4, rho, out1, (4, 3 - rho), in2, (0, 3 - rho), 17 + rho, partner, even)

    def send_in3(rho):
        start(5, rho, out2, (4, 3 - rho), in3, (0, 3 - rho), 13 + rho, partner, even)

    def have_out1(rho):
        arrived(0, rho, out1, (0, 3 - rho), 21 + rho, even)

    def have_out2(rho):
        arrived(1, rho, out2, (0, 4), 16, even)

    def have_out2_trace(rho):
        arrived(6, rho, out2, (16, 3 - rho), rho + 1, even)

    def have_out3(rho):
        arrived(2, rho, out3, (0, 3 - rho), 13 + rho, even)

    def have_in1(rho):
        arrived(3, rho, in1, (0, 3 - rho), 21 + rho, odd)

    def have_in2(rho):
        arrived(4, rho, in2, (0, 3 - rho), 17 + rho, odd)

    def have_in3(rho):
        arrived(5, rho, in3, (0, 3 - rho), 13 + rho, odd)

    def pass_on(j, src, device):
        c = pltpu.make_async_remote_copy(
            src_ref=src,
            dst_ref=got.at[j],
            send_sem=sum_send_sem.at[j],
            recv_sem=sum_recv_sem.at[j],
            device_id=device,
            device_id_type=MESH,
        )
        c.start()
        sends["sum", j] = c

    def received(j):
        pltpu.make_async_copy(got.at[j], got.at[j], sum_recv_sem.at[j]).wait()

    def product(buf, lo, hi, left, delta, first=False):
        a0 = REACH + 4 * delta * (1 - 2 * left)
        c0 = (1 - left) * 4 * delta

        def step(t, carry):
            c = 2 * t
            lhs = jnp.concatenate([own[:, a0 + r].reshape(R * BS, BS) for r in range(R)], axis=1)
            rhs = jnp.concatenate([buf[:, c].reshape(R * BS, BS), buf[:, c + 1].reshape(R * BS, BS)], axis=1)
            res = jnp.dot(lhs, rhs, preferred_element_type=jnp.float32)
            for h in range(2):
                part = res[:, h * BS:(h + 1) * BS].reshape(R, BS, BS)
                if first:
                    acc[:, c0 + c + h] = part
                else:
                    acc[:, c0 + c + h] += part
            return carry

        lax.fori_loop(lo // 2, hi // 2, step, 0)

    def spread_for_out1(rho):
        spread(odd * rho + even * (R - 1 - rho))

    for c in loads:
        c.wait()
    spread_for_out1(3)
    spread_for_out1(2)
    pl.semaphore_wait(barrier, len(greeted))
    send_out1(3)
    spread_for_out1(1)
    send_out1(2)
    spread_for_out1(0)
    send_out1(1)
    for rho in (3, 2):
        send_in1(rho)
    send_out1(0)
    for rho in ORDER:
        send_out2_trace(rho)
    for rho in (1, 0):
        send_in1(rho)

    product(own, 0, 28, even, 0, first=True)
    for rho in ORDER:
        have_in1(rho)
    product(in1, 0, 24, odd, 1)

    for rho in ORDER:
        have_out1(rho)
        send_in2(rho)
    send_out3(3)
    send_out2(3)
    product(out1, 0, 24, even, 1)
    for rho in ORDER:
        have_out2_trace(rho)
    for rho in ORDER:
        have_in2(rho)

    total = sum(acc[r, REACH + r] for r in range(R))
    for r in range(R):
        a = [out1[even * r + odd * q, even * (16 + q) + odd * (4 + r)] for q in range(R)]
        b = [in1[even * q + odd * r, even * (4 + r) + odd * (16 + q)] for q in range(R)]
        total += 2.0 * jnp.dot(
            jnp.concatenate(a, axis=1), jnp.concatenate(b, axis=0), preferred_element_type=jnp.float32
        )
    for r in range(R):
        a = [out1[even * r + odd * q, even * (20 + q) + odd * r] for q in range(r + 1)]
        b = [in2[even * q + odd * r, even * r + odd * (16 + q)] for q in range(r + 1)]
        a += [out2[even * r + odd * q, even * (16 + q) + odd * r] for q in range(r + 1)]
        b += [in1[even * q + odd * r, even * r + odd * (20 + q)] for q in range(r + 1)]
        total += jnp.dot(
            jnp.concatenate(a, axis=1), jnp.concatenate(b, axis=0), preferred_element_type=jnp.float32
        )
    rows = lax.broadcasted_iota(jnp.int32, (BS, BS), 0)
    lanes = lax.broadcasted_iota(jnp.int32, (BS, BS), 1)
    total = jnp.where(rows == lanes, total, 0.0)
    sent[0] = jnp.sum(total.reshape(BS // 8, 8, BS), axis=0)

    product(in2, 0, 4, odd, 2)
    pass_on(0, sent.at[0], partner)
    product(in2, 4, 8, odd, 2)
    received(0)
    sent[1] = sent[0] + got[0]
    product(in2, 8, 10, odd, 2)
    queue = [
        lambda: send_out2(2),
        lambda: send_out2(1),
        lambda: (send_out2(0), send_out3(2), send_out3(1), send_out3(0)),
    ]
    work = [
        lambda: product(in2, 10, 18, odd, 2),
        lambda: [(have_out2(rho), send_in3(rho)) for rho in (3, 2)],
        lambda: [(have_out2(rho), send_in3(rho)) for rho in (1, 0)],
    ]
    fill = [lambda: product(in2, 18, 20, odd, 2)]
    def add_up(j, at, group):
        values = [sent[1 + j]]
        for k in range(len(group)):
            received(at + k)
            values.append(got[at + k])
        while len(values) > 1:
            values = [values[i] + values[i + 1] for i in range(0, len(values), 2)]
        sent[2 + j] = values[0]

    before = [(2, 3), (1, 3), (1, 2)]
    for rho in ORDER:
        wait_sent(0, rho)
        wait_sent(6, rho)
    at = 1
    for j, group in enumerate(groups):
        wait_sent(*before[j])
        for k, d in enumerate(group):
            pass_on(at + k, sent.at[1 + j], d)
        for q in queue[j:] if j == len(groups) - 1 else queue[j:j + 1]:
            q()
        for w in work[j:] if j == len(groups) - 1 else work[j:j + 1]:
            w()
        if j < len(groups) - 1:
            add_up(j, at, group)
            for f in fill[j:j + 1]:
                f()
        at += len(group)
    last = 1 + len(groups)
    product(out2, 0, 20, even, 2)
    for rho in ORDER:
        have_in3(rho)
    product(in3, 0, 16, odd, 3)

    for rho in ORDER:
        if rho == 0:
            add_up(len(groups) - 1, at - len(groups[-1]), groups[-1])
            trace_ref[0, 0] = jnp.sum(sent[last]) * (1.0 / (n * R * BS))
        have_out3(rho)
        row = even * rho + odd * (R - 1 - rho)
        top = odd * (R - 1 - rho)
        a0 = REACH + 12 * (1 - 2 * even) + row
        m = rho + 1
        begin = odd * (1 if rho < 2 else 0)
        c0 = odd * 12

        def step(t, carry, rho=rho, row=row, top=top, a0=a0, m=m, c0=c0):
            c = 2 * t
            lhs = own[pl.ds(top, m), a0].reshape(m * BS, BS)
            rhs = jnp.concatenate([out3[row, c], out3[row, c + 1]], axis=1)
            res = jnp.dot(lhs, rhs, preferred_element_type=jnp.float32)
            for h in range(2):
                acc[pl.ds(top, m), c0 + c + h] += res[:, h * BS:(h + 1) * BS].reshape(m, BS, BS)
            return carry

        lax.fori_loop(begin, begin + (7 if rho < 2 else 8), step, 0)
        done = even * rho + odd * (R - 1 - rho)

        def take(s, carry, done=done):
            p = position(done, s)
            tile = acc[done, jnp.clip(p, 0, COLS - 1)]
            square_ref[done, s] = jnp.where(p >= 0, tile, 0.0).astype(jnp.bfloat16)
            return carry

        lax.fori_loop(0, slots, take, 0)

    for c in sends.values():
        c.wait_send()


def shards(tiles, columns, n_blk, n_grp):
    n = n_blk * n_grp
    slots = tiles.shape[1]
    steps = 1 + sum(len(group) for group in xor_groups(n))
    piece = lambda delta: pltpu.VMEM((R, COLS - 4 * delta, BS, BS), jnp.bfloat16)
    square, trace_mean = pl.pallas_call(
        functools.partial(square_kernel, n_blk, n_grp),
        out_shape=(
            jax.ShapeDtypeStruct(tiles.shape, jnp.bfloat16),
            jax.ShapeDtypeStruct((1, 1), jnp.float32),
        ),
        in_specs=[
            pl.BlockSpec(memory_space=pltpu.HBM),
            pl.BlockSpec(memory_space=pltpu.HBM),
        ],
        out_specs=(pl.BlockSpec(memory_space=pltpu.VMEM), pl.BlockSpec(memory_space=pltpu.SMEM)),
        scratch_shapes=[
            pltpu.SMEM(columns.shape, jnp.int32),
            pltpu.VMEM(tiles.shape, jnp.bfloat16),
            piece(0),
            piece(1), piece(2), piece(3), piece(1), piece(2), piece(3),
            pltpu.VMEM((R, COLS, BS, BS), jnp.float32),
            pltpu.VMEM((steps, 8, BS), jnp.float32),
            pltpu.VMEM((steps, 8, BS), jnp.float32),
            pltpu.SemaphoreType.DMA((2,)),
            pltpu.SemaphoreType.DMA((7, R)),
            pltpu.SemaphoreType.DMA((7, R)),
            pltpu.SemaphoreType.DMA((steps,)),
            pltpu.SemaphoreType.DMA((steps,)),
        ],
        compiler_params=pltpu.CompilerParams(
            collective_id=0, has_side_effects=True, vmem_limit_bytes=36 * 2**20
        ),
    )(pltpu.with_memory_space_constraint(columns, pltpu.HBM), pltpu.with_memory_space_constraint(tiles, pltpu.HBM))
    return square, trace_mean[0, 0]


def solution(mesh):
    n_blk, n_grp = mesh.shape["blk"], mesh.shape["grp"]
    return jax.shard_map(
        functools.partial(shards, n_blk=n_blk, n_grp=n_grp),
        mesh=mesh,
        in_specs=(P(("blk", "grp"), None, None, None), P(("blk", "grp"), None)),
        out_specs=(P(("blk", "grp"), None, None, None), P()),
        check_vma=False,
    )
```

```python
import functools

import jax
import jax.numpy as jnp
from jax import lax
from jax.experimental import pallas as pl
from jax.experimental.pallas import tpu as pltpu
from jax.sharding import PartitionSpec as P

REACH = 12
R = 4
BS = 128
COLS = 2 * REACH + R
MESH = pl.DeviceIdType.MESH
ORDER = (3, 2, 1, 0)


def xor_groups(n):
    groups = []
    for bits in ((2, 4), (8, 64, 128), (16, 32)):
        bits = [w for w in bits if w < n]
        if bits:
            groups.append([sum(w for i, w in enumerate(bits) if k >> i & 1) for k in range(1, 2 ** len(bits))])
    return groups


def square_kernel(n_blk, n_grp, columns_hbm, tiles_hbm, square_ref, trace_ref,
                  columns_ref, across_vmem, across_ref, tiles, own, raw3, raw2, raw1, raw0,
                  out1, out2, out3, in1, in2, in3, acc, sent, got,
                  load_sem, send_sem, recv_sem, sum_send_sem, sum_recv_sem):
    n = n_blk * n_grp
    slots = tiles.shape[1]
    me = lax.axis_index("blk") * n_grp + lax.axis_index("grp")
    odd = lax.rem(me, 2)
    even = 1 - odd
    sign = 2 * odd - 1

    loads = [
        pltpu.make_async_copy(columns_hbm, columns_ref, load_sem.at[0]),
        pltpu.make_async_copy(tiles_hbm, tiles, load_sem.at[1]),
    ]
    for c in loads:
        c.start()

    def coords(d):
        return (d // n_grp, lax.rem(d, n_grp))

    def dev(offset):
        return coords(lax.rem(me + offset + n, n))

    partner = dev(-sign)
    across = dev(sign)
    onward = dev(-2 * sign)
    behind = dev(2 * sign)

    def mirror(mask):
        d = me
        w = 1
        while w < n:
            if mask & w:
                d += w * (1 - 2 * lax.rem(me // w, 2))
            w *= 2
        return coords(d)

    groups = [[mirror(mask) for mask in group] for group in xor_groups(n)]

    barrier = pltpu.get_barrier_semaphore()
    greeted = [partner, across, onward, behind] + sum(groups, [])
    for d in greeted:
        pl.semaphore_signal(barrier, inc=1, device_id=d, device_id_type=MESH)

    zero = jnp.zeros((BS, BS), jnp.bfloat16)
    raw = {3: raw3, 2: raw2, 1: raw1, 0: raw0}
    for buf, delta, left in ((out2, 2, even), (out3, 3, even),
                             (in1, 1, odd), (in2, 2, odd), (in3, 3, odd)):
        for rho in range(R - 1):
            row = left * rho + (1 - left) * (R - 1 - rho)
            first = left * (25 - 4 * delta + rho)
            for e in range(R - 1 - rho):
                buf[row, first + e] = zero

    def position(columns, r, s):
        column = columns[r, s]
        p = column - me * R + REACH
        p = jnp.where(p < 0, p + n * R, p)
        p = jnp.where(p >= n * R, p - n * R, p)
        return jnp.where(column >= 0, p, -1)

    def spread(columns, r, source, target, first, count):
        filled = [position(columns, r, s) for s in range(slots)]

        def place(p, carry):
            s = 0
            for k, f in enumerate(filled):
                s = jnp.where(f == p + first, k + 1, s)
            tile = source(jnp.maximum(s - 1, 0))
            target[r, p] = jnp.where(s > 0, tile, zero)
            return carry

        def place_some(g, carry):
            for e in range(4):
                place(4 * g + e, carry)
            return carry

        lax.fori_loop(0, count // 4, place_some, 0)

    sends = {}

    def start(k, rho, src, first, dst, to, length, device, left):
        row = left * rho + (1 - left) * (R - 1 - rho)
        c = pltpu.make_async_remote_copy(
            src_ref=src.at[row, pl.ds(left * first[0] + (1 - left) * first[1], length)],
            dst_ref=dst.at[row, pl.ds(left * to[0] + (1 - left) * to[1], length)],
            send_sem=send_sem.at[k, rho],
            recv_sem=recv_sem.at[k, rho],
            device_id=device,
            device_id_type=MESH,
        )
        c.start()
        sends[k, rho] = c

    def wait_sent(k, rho):
        sends.pop((k, rho)).wait_send()

    def arrived(k, rho, buf, to, length, left):
        row = left * rho + (1 - left) * (R - 1 - rho)
        here = buf.at[row, pl.ds(left * to[0] + (1 - left) * to[1], length)]
        pltpu.make_async_copy(here, here, recv_sem.at[k, rho]).wait()

    def send_out1(rho):
        c = pltpu.make_async_remote_copy(
            src_ref=tiles_hbm.at[odd * rho + even * (R - 1 - rho)],
            dst_ref=raw[rho],
            send_sem=send_sem.at[0, rho],
            recv_sem=recv_sem.at[0, rho],
            device_id=across,
            device_id_type=MESH,
        )
        c.start()
        sends[0, rho] = c

    def send_in1(rho):
        start(3, rho, own, (4, 3 - rho), in1, (0, 3 - rho), 21 + rho, partner, even)

    def send_out2(rho):
        start(1, rho, own, (8, 4), out2, (0, 4), 16, onward, even)

    def send_out2_trace(rho):
        start(6, rho, own, (24, 3 - rho), out2, (16, 3 - rho), rho + 1, onward, even)

    def send_out3(rho):
        start(2, rho, out1, (8, 3 - rho), out3, (0, 3 - rho), 13 + rho, onward, even)

    def send_in2(rho):
        start(4, rho, out1, (4, 3 - rho), in2, (0, 3 - rho), 17 + rho, partner, even)

    def send_in3(rho):
        start(5, rho, out2, (4, 3 - rho), in3, (0, 3 - rho), 13 + rho, partner, even)

    def have_out1(rho):
        pltpu.make_async_copy(raw[rho], raw[rho], recv_sem.at[0, rho]).wait()
        row = even * rho + odd * (R - 1 - rho)
        spread(across_ref, row, lambda s: raw[rho][s], out1, odd * 4, COLS - 4)

    def have_out2(rho):
        arrived(1, rho, out2, (0, 4), 16, even)

    def have_out2_trace(rho):
        arrived(6, rho, out2, (16, 3 - rho), rho + 1, even)

    def have_out3(rho):
        arrived(2, rho, out3, (0, 3 - rho), 13 + rho, even)

    def have_in1(rho):
        arrived(3, rho, in1, (0, 3 - rho), 21 + rho, odd)

    def have_in2(rho):
        arrived(4, rho, in2, (0, 3 - rho), 17 + rho, odd)

    def have_in3(rho):
        arrived(5, rho, in3, (0, 3 - rho), 13 + rho, odd)

    def pass_on(j, src, device):
        c = pltpu.make_async_remote_copy(
            src_ref=src,
            dst_ref=got.at[j],
            send_sem=sum_send_sem.at[j],
            recv_sem=sum_recv_sem.at[j],
            device_id=device,
            device_id_type=MESH,
        )
        c.start()
        sends["sum", j] = c

    def received(j):
        pltpu.make_async_copy(got.at[j], got.at[j], sum_recv_sem.at[j]).wait()

    def product(buf, lo, hi, left, delta, first=False):
        a0 = REACH + 4 * delta * (1 - 2 * left)
        c0 = (1 - left) * 4 * delta

        def step(t, carry):
            c = 2 * t
            lhs = jnp.concatenate([own[:, a0 + r].reshape(R * BS, BS) for r in range(R)], axis=1)
            rhs = jnp.concatenate([buf[:, c].reshape(R * BS, BS), buf[:, c + 1].reshape(R * BS, BS)], axis=1)
            res = jnp.dot(lhs, rhs, preferred_element_type=jnp.float32)
            for h in range(2):
                part = res[:, h * BS:(h + 1) * BS].reshape(R, BS, BS)
                if first:
                    acc[:, c0 + c + h] = part
                else:
                    acc[:, c0 + c + h] += part
            return carry

        lax.fori_loop(lo // 2, hi // 2, step, 0)

    pl.semaphore_wait(barrier, len(greeted))
    c = pltpu.make_async_remote_copy(
        src_ref=columns_hbm,
        dst_ref=across_vmem,
        send_sem=send_sem.at[7, 0],
        recv_sem=recv_sem.at[7, 0],
        device_id=across,
        device_id_type=MESH,
    )
    c.start()
    sends[7, 0] = c
    for rho in ORDER:
        send_out1(rho)
    for c in loads:
        c.wait()
    for rho in ORDER:
        r = odd * rho + even * (R - 1 - rho)
        spread(columns_ref, r, lambda s, r=r: tiles[r, s], own, 0, COLS)
    pltpu.make_async_copy(across_vmem, across_vmem, recv_sem.at[7, 0]).wait()
    c = pltpu.make_async_copy(across_vmem, across_ref, load_sem.at[2])
    c.start()
    c.wait()
    for rho in ORDER:
        send_out2_trace(rho)
    send_out2(3)
    for rho in ORDER:
        send_in1(rho)

    product(own, 0, 28, even, 0, first=True)
    for rho in ORDER:
        have_in1(rho)
    product(in1, 0, 24, odd, 1)

    for rho in ORDER:
        have_out1(rho)
        if rho < 3:
            send_in2(rho + 1)
    send_out3(3)
    send_in2(0)
    product(out1, 0, 24, even, 1)
    for rho in ORDER:
        have_out2_trace(rho)
    for rho in ORDER:
        have_in2(rho)

    total = sum(acc[r, REACH + r] for r in range(R))
    for r in range(R):
        a = [out1[even * r + odd * q, even * (16 + q) + odd * (4 + r)] for q in range(R)]
        b = [in1[even * q + odd * r, even * (4 + r) + odd * (16 + q)] for q in range(R)]
        total += 2.0 * jnp.dot(
            jnp.concatenate(a, axis=1), jnp.concatenate(b, axis=0), preferred_element_type=jnp.float32
        )
    for r in range(R):
        a = [out1[even * r + odd * q, even * (20 + q) + odd * r] for q in range(r + 1)]
        b = [in2[even * q + odd * r, even * r + odd * (16 + q)] for q in range(r + 1)]
        a += [out2[even * r + odd * q, even * (16 + q) + odd * r] for q in range(r + 1)]
        b += [in1[even * q + odd * r, even * r + odd * (20 + q)] for q in range(r + 1)]
        total += jnp.dot(
            jnp.concatenate(a, axis=1), jnp.concatenate(b, axis=0), preferred_element_type=jnp.float32
        )
    rows = lax.broadcasted_iota(jnp.int32, (BS, BS), 0)
    lanes = lax.broadcasted_iota(jnp.int32, (BS, BS), 1)
    total = jnp.where(rows == lanes, total, 0.0)
    sent[0] = jnp.sum(total.reshape(BS // 8, 8, BS), axis=0)

    product(in2, 0, 4, odd, 2)
    pass_on(0, sent.at[0], partner)
    product(in2, 4, 8, odd, 2)
    received(0)
    sent[1] = sent[0] + got[0]
    product(in2, 8, 10, odd, 2)
    queue = [
        lambda: send_out2(2),
        lambda: send_out2(1),
        lambda: (send_out2(0), send_out3(2), send_out3(1), send_out3(0)),
    ]
    work = [
        lambda: product(in2, 10, 18, odd, 2),
        lambda: [(have_out2(rho), send_in3(rho)) for rho in (3, 2)],
        lambda: [(have_out2(rho), send_in3(rho)) for rho in (1, 0)],
    ]
    fill = [lambda: product(in2, 18, 20, odd, 2)]
    def add_up(j, at, group):
        values = [sent[1 + j]]
        for k in range(len(group)):
            received(at + k)
            values.append(got[at + k])
        while len(values) > 1:
            values = [values[i] + values[i + 1] for i in range(0, len(values), 2)]
        sent[2 + j] = values[0]

    before = [(1, 3), (2, 3), (1, 2)]
    for rho in ORDER:
        wait_sent(0, rho)
        wait_sent(6, rho)
    at = 1
    for j, group in enumerate(groups):
        wait_sent(*before[j])
        for k, d in enumerate(group):
            pass_on(at + k, sent.at[1 + j], d)
        for q in queue[j:] if j == len(groups) - 1 else queue[j:j + 1]:
            q()
        for w in work[j:] if j == len(groups) - 1 else work[j:j + 1]:
            w()
        if j < len(groups) - 1:
            add_up(j, at, group)
            for f in fill[j:j + 1]:
                f()
        at += len(group)
    last = 1 + len(groups)
    product(out2, 0, 20, even, 2)
    for rho in ORDER:
        have_in3(rho)
    product(in3, 0, 16, odd, 3)

    for rho in ORDER:
        if rho == 0:
            add_up(len(groups) - 1, at - len(groups[-1]), groups[-1])
            trace_ref[0, 0] = jnp.sum(sent[last]) * (1.0 / (n * R * BS))
        have_out3(rho)
        row = even * rho + odd * (R - 1 - rho)
        top = odd * (R - 1 - rho)
        a0 = REACH + 12 * (1 - 2 * even) + row
        m = rho + 1
        begin = odd * (1 if rho < 2 else 0)
        c0 = odd * 12

        def step(t, carry, rho=rho, row=row, top=top, a0=a0, m=m, c0=c0):
            c = 2 * t
            lhs = own[pl.ds(top, m), a0].reshape(m * BS, BS)
            rhs = jnp.concatenate([out3[row, c], out3[row, c + 1]], axis=1)
            res = jnp.dot(lhs, rhs, preferred_element_type=jnp.float32)
            for h in range(2):
                acc[pl.ds(top, m), c0 + c + h] += res[:, h * BS:(h + 1) * BS].reshape(m, BS, BS)
            return carry

        if rho < 2:
            for t in range(7):
                step(begin + t, 0)
        else:
            lax.fori_loop(0, 8, step, 0)
        done = even * rho + odd * (R - 1 - rho)

        def take(s, carry, done=done):
            p = position(columns_ref, done, s)
            tile = acc[done, jnp.clip(p, 0, COLS - 1)]
            square_ref[done, s] = jnp.where(p >= 0, tile, 0.0).astype(jnp.bfloat16)
            return carry

        def take_some(g, carry, take=take):
            for e in range(5):
                take(5 * g + e, carry)
            return carry

        lax.fori_loop(0, slots // 5, take_some, 0)
        for t in range(slots // 5 * 5, slots):
            take(t, 0)

    for c in sends.values():
        c.wait_send()


def shards(tiles, columns, n_blk, n_grp):
    n = n_blk * n_grp
    slots = tiles.shape[1]
    steps = 1 + sum(len(group) for group in xor_groups(n))
    piece = lambda delta: pltpu.VMEM((R, COLS - 4 * delta, BS, BS), jnp.bfloat16)
    square, trace_mean = pl.pallas_call(
        functools.partial(square_kernel, n_blk, n_grp),
        out_shape=(
            jax.ShapeDtypeStruct(tiles.shape, jnp.bfloat16),
            jax.ShapeDtypeStruct((1, 1), jnp.float32),
        ),
        in_specs=[
            pl.BlockSpec(memory_space=pltpu.HBM),
            pl.BlockSpec(memory_space=pltpu.HBM),
        ],
        out_specs=(pl.BlockSpec(memory_space=pltpu.VMEM), pl.BlockSpec(memory_space=pltpu.SMEM)),
        scratch_shapes=[
            pltpu.SMEM(columns.shape, jnp.int32),
            pltpu.VMEM(columns.shape, jnp.int32),
            pltpu.SMEM(columns.shape, jnp.int32),
            pltpu.VMEM(tiles.shape, jnp.bfloat16),
            piece(0),
        ] + [pltpu.VMEM(tiles.shape[1:], jnp.bfloat16)] * R + [
            piece(1), piece(2), piece(3), piece(1), piece(2), piece(3),
            pltpu.VMEM((R, COLS, BS, BS), jnp.float32),
            pltpu.VMEM((steps, 8, BS), jnp.float32),
            pltpu.VMEM((steps, 8, BS), jnp.float32),
            pltpu.SemaphoreType.DMA((3,)),
            pltpu.SemaphoreType.DMA((8, R)),
            pltpu.SemaphoreType.DMA((8, R)),
            pltpu.SemaphoreType.DMA((steps,)),
            pltpu.SemaphoreType.DMA((steps,)),
        ],
        compiler_params=pltpu.CompilerParams(
            collective_id=0, has_side_effects=True, vmem_limit_bytes=40 * 2**20
        ),
    )(pltpu.with_memory_space_constraint(columns, pltpu.HBM), pltpu.with_memory_space_constraint(tiles, pltpu.HBM))
    return square, trace_mean[0, 0]


def solution(mesh):
    n_blk, n_grp = mesh.shape["blk"], mesh.shape["grp"]
    return jax.shard_map(
        functools.partial(shards, n_blk=n_blk, n_grp=n_grp),
        mesh=mesh,
        in_specs=(P(("blk", "grp"), None, None, None), P(("blk", "grp"), None)),
        out_specs=(P(("blk", "grp"), None, None, None), P()),
        check_vma=False,
    )
```
